256 devices in a mesh: gx: 32 (over x_hi, z, core), gy: 8 (over y, x_lo).
Axes of the slice: x: 4 (x_hi: 2, x_lo: 2; x = x_hi * 2 + x_lo), y: 4, z: 8, core: 2. Of those that a mesh axis runs over, the one named last changes fastest.
Arguments:
- adjoint_out: bfloat16 [1024, 4096, 128], P('gx', 'gy'), may hold values from -6 to 6
- shift_x: int32 [128], replicated, may hold values from -8 to 8, as said below
- shift_y: int32 [128], replicated, may hold values from -8 to 8, as said below
- frac_x: float32 [128], replicated, may hold values from 0 to 1
- frac_y: float32 [128], replicated, may hold values from 0 to 1
Outputs:
- adjoint_in: float32 [1024, 4096, 128], P('gx', 'gy')
The draws below stay inside these ranges and needn't reach their ends.
Inputs may be any that keep to these rules, and one draw needn't show every extreme that they name: `shift_x`: signed cell shift of each velocity along x; both 8 and -8 occur. `shift_y`: signed cell shift of each velocity along y; both 8 and -8 occur.
All inputs are finite; a program needn't handle non-finite values.
Results may differ from the reference program's by a relative error of at most 0.0003.
Values may be sent and summed in bfloat16 or wider, within the bound.
A program may use at most 64 MiB of HBM per device.

```python
import math
import jax
import jax.numpy as jnp
from jax import lax

V = 128
REACH = 8
NX = 1024
NY = 4096


def shift_table(key):
    first, second = jax.random.split(key)
    base = jax.random.randint(first, (V,), -REACH, REACH + 1, dtype=jnp.int32)
    order = jax.random.permutation(second, V)
    base = base.at[order[0]].set(REACH)
    base = base.at[order[1]].set(-REACH)
    return base.astype(jnp.int32)


def draw_shift_x(key, part):
    return shift_table(jax.random.fold_in(key, 11))


def draw_shift_y(key, part):
    return shift_table(jax.random.fold_in(key, 23))


def shard_levels(stream_key, dims, cuts, smallest, high):
    loudness = 1.0
    for dim, parts in cuts:
        draws = jax.random.uniform(jax.random.fold_in(jax.random.fold_in(stream_key, 6), dim), (parts,), jnp.float32, smallest / len(cuts), high / len(cuts))
        loudness = loudness * jnp.repeat(jnp.exp(draws), dims[dim] // parts).reshape((-1,) + (1,) * (len(dims) - 1 - dim))
    return loudness


def scatter_about(own_key, shape, width, most, cuts=(), kind=jnp.bfloat16):
    level = shard_levels(own_key, shape, cuts, -0.22, 0.18) if cuts else 1.0
    entries = jax.random.normal(own_key, shape, jnp.float32) * width * level
    return jnp.minimum(jnp.maximum(entries, -most), most).astype(kind)


def setup_inputs(seed: int = 0) -> dict:
    keys = jax.random.split(jax.random.key(seed), 6)
    adjoint_out = scatter_about(keys[0], (NX, NY, V), 1.0, 6.0, ((0, 32), (1, 8)))
    shift_x = draw_shift_x(jax.random.fold_in(keys[5], 71), 0)
    shift_y = draw_shift_y(jax.random.fold_in(keys[5], 71), 0)
    frac_x = jnp.clip(jax.random.uniform(keys[3], (V,), jnp.float32, 0.0, 1.0), 0.0, 1.0)
    frac_y = jnp.clip(jax.random.uniform(keys[4], (V,), jnp.float32, 0.0, 1.0), 0.0, 1.0)
    return dict(adjoint_out=adjoint_out, shift_x=shift_x, shift_y=shift_y, frac_x=frac_x, frac_y=frac_y)


def coef_table(shift, frac):
    t = frac.astype(jnp.float32)
    weights = jnp.stack([-t * (t - 1.0) * (t - 2.0) / 6.0, (t + 1.0) * (t - 1.0) * (t - 2.0) / 2.0, -(t + 1.0) * t * (t - 2.0) / 2.0, (t + 1.0) * t * (t - 1.0) / 6.0])
    offsets = jnp.arange(2 * REACH + 4, dtype=jnp.int32) - (REACH + 2)
    taps = jnp.arange(4, dtype=jnp.int32)
    hits = (shift.astype(jnp.int32)[None, None, :] - taps[None, :, None] + 1) == offsets[:, None, None]
    return jnp.sum(jnp.where(hits, weights[None, :, :], jnp.zeros_like(weights[None, :, :])), axis=1)


def reference(adjoint_out, shift_x, shift_y, frac_x, frac_y):
    coef_x = coef_table(shift_x, frac_x)
    coef_y = coef_table(shift_y, frac_y)
    block = math.gcd(V, 16)
    starts = jnp.arange(V // block, dtype=jnp.int32) * block

    def one_block(start):
        sub = lax.dynamic_slice_in_dim(adjoint_out, start, block, 2).astype(jnp.float32)
        cy = lax.dynamic_slice_in_dim(coef_y, start, block, 1)
        cx = lax.dynamic_slice_in_dim(coef_x, start, block, 1)
        middle = jnp.zeros(sub.shape, jnp.float32)
        for index in range(2 * REACH + 4):
            offset = index - (REACH + 2)
            middle = middle + cy[index][None, None, :] * jnp.roll(sub, -offset, axis=1)
        result = jnp.zeros(sub.shape, jnp.float32)
        for index in range(2 * REACH + 4):
            offset = index - (REACH + 2)
            result = result + cx[index][None, None, :] * jnp.roll(middle, -offset, axis=0)
        return result

    blocks = lax.map(one_block, starts)
    return jnp.moveaxis(blocks, 0, 2).reshape(NX, NY, V)
```

```python
import functools
import jax
import jax.numpy as jnp
from jax import lax
from jax.experimental import pallas as pl
from jax.experimental.pallas import tpu as pltpu
from jax.sharding import PartitionSpec as P

REACH = 8
TOP = REACH + 2
BOT = REACH + 1
PAD = 16
LANES = 128
STEP = 128
MESH = pl.DeviceIdType.MESH


def lagrange(t):
    return (
        -t * (t - 1.0) * (t - 2.0) / 6.0,
        (t + 1.0) * (t - 1.0) * (t - 2.0) / 2.0,
        -(t + 1.0) * t * (t - 2.0) / 2.0,
        (t + 1.0) * t * (t - 1.0) / 6.0,
    )


def rows_needed(shift):
    return jnp.clip(2 - shift, 0, TOP), jnp.clip(shift + 1, 0, BOT)


def build_table(table, shift, count, depth, slots):
    f32 = jnp.float32
    need = count.astype(f32)
    wide = jnp.broadcast_to(need, (16, LANES))
    level = lax.broadcasted_iota(jnp.int32, (16, LANES), 0).astype(f32)
    inside = wide > level
    before = jnp.sum(jnp.minimum(wide, level), axis=1, keepdims=True)
    row = lax.broadcasted_iota(jnp.int32, (LANES, LANES), 0)
    col = lax.broadcasted_iota(jnp.int32, (LANES, LANES), 1)
    upper = jnp.where(row < col, 1.0, 0.0).astype(jnp.bfloat16)
    rank = jnp.dot(
        jnp.where(inside, 1.0, 0.0).astype(jnp.bfloat16), upper, preferred_element_type=f32
    )
    place = jnp.where(inside, before + rank, -1.0)
    lane = row.astype(f32)
    for h in range(depth):
        line = jnp.broadcast_to(place[h : h + 1, :], (LANES, LANES))
        for p in range(slots):
            hit = jnp.where(line == lane + float(p * LANES), 1.0, 0.0)
            table[p * LANES : (p + 1) * LANES, h * LANES : (h + 1) * LANES] = hit.astype(jnp.bfloat16)


def x_tile(xs, mid, y, unit, wx, first, last, low, high):
    m16 = unit >= 16.0
    m8 = unit >= 8.0
    left = jnp.where(m16, unit - 16.0, jnp.where(m8, unit - 8.0, unit))
    m4 = left >= 4.0
    left = jnp.where(m4, left - 4.0, left)
    m2 = left >= 2.0
    left = jnp.where(m2, left - 2.0, left)
    m1 = left >= 1.0

    def source(r):
        return xs[min(max(r, low), high), pl.ds(y, 16), :]

    @functools.cache
    def by8(j):
        return jnp.where(m16, source(j + 16), jnp.where(m8, source(j + 8), source(j)))

    @functools.cache
    def by4(j):
        return jnp.where(m4, by8(j + 4), by8(j))

    @functools.cache
    def by2(j):
        return jnp.where(m2, by4(j + 2), by4(j))

    @functools.cache
    def by1(j):
        return jnp.where(m1, by2(j + 1), by2(j)).astype(jnp.float32)

    for i in range(first, last):
        mid[i, pl.ds(y, 16), :] = (
            wx[0] * by1(i + 3) + wx[1] * by1(i + 2) + wx[2] * by1(i + 1) + wx[3] * by1(i)
        )


def y_row(mid, out, i, start, count, strip, turn, minus, plus, wy):
    tiles = count // 8
    base = start + PAD

    @functools.cache
    def turned(j):
        return jnp.take_along_axis(mid[i, pl.ds(base + 8 * j, 8), :], turn, axis=0)

    for j in range(-1, tiles + 1):
        strip[pl.ds(8 * (j + 1), 8), :] = jnp.where(
            minus, turned(j - 1), jnp.where(plus, turned(j + 1), turned(j))
        )
    for j in range(tiles):
        b = 8 * (j + 1)
        out[i, pl.ds(start + 8 * j, 8), :] = (
            wy[0] * strip[pl.ds(b + 1, 8), :]
            + wy[1] * strip[pl.ds(b, 8), :]
            + wy[2] * strip[pl.ds(b - 1, 8), :]
            + wy[3] * strip[pl.ds(b - 2, 8), :]
        )


def kernel(dims, slots, x_hbm, sx_ref, sy_ref, fx_ref, fy_ref, out, xs, mid, strip, *rest):
    rows, cols, nx, ny = dims
    if slots:
        table, send, recv, load_sem, x_send, x_recv, y_send, y_recv, c_send, c_recv = rest
    else:
        load_sem, x_send, x_recv, y_send, y_recv, c_send, c_recv = rest
    gx, gy = lax.axis_index("gx"), lax.axis_index("gy")
    xm, xp = lax.rem(gx + nx - 1, nx), lax.rem(gx + 1, nx)
    ym, yp = lax.rem(gy + ny - 1, ny), lax.rem(gy + 1, ny)

    loads = [
        pltpu.make_async_copy(x_hbm.at[pl.ds(a, n)], xs.at[pl.ds(TOP + a, n), pl.ds(PAD, cols), :], load_sem.at[k])
        for k, (a, n) in enumerate(((rows - TOP, TOP), (0, TOP), (TOP, rows - 2 * TOP)))
    ]
    for load in loads:
        load.start()
    barrier = pltpu.get_barrier_semaphore()
    for a in (xm, gx, xp):
        for b in (ym, gy, yp):
            if a is gx and b is gy:
                continue
            pl.semaphore_signal(barrier, inc=1, device_id=(a, b), device_id_type=MESH)

    counts = rows_needed(sx_ref[...])
    if slots:
        for d in range(2):
            build_table(table.at[d], sx_ref[...], counts[d], (TOP, BOT)[d], slots)
    unit = jnp.broadcast_to((sx_ref[...] + REACH).astype(jnp.float32), (16, LANES)).astype(jnp.bfloat16)
    wx = [jnp.broadcast_to(w, (16, LANES)) for w in lagrange(fx_ref[...])]
    wy = [jnp.broadcast_to(w, (8, LANES)) for w in lagrange(fy_ref[...])]
    tot = lax.broadcasted_iota(jnp.int32, (8, LANES), 0) + jnp.broadcast_to(sy_ref[...], (8, LANES))
    turn, minus, plus = (tot + 16) & 7, tot < 0, tot >= 8

    edges = [0] + [STEP * (k + 1) + PAD for k in range(cols // STEP - 1)] + [cols]
    n = len(edges) - 1
    mine = ([rows - 1 - h + TOP for h in range(TOP)], [TOP + h for h in range(BOT)])
    theirs = ([TOP - 1 - h for h in range(TOP)], [TOP + rows + h for h in range(BOT)])

    def pack(k):
        a, w = edges[k], edges[k + 1] - edges[k]
        for d in range(2):
            block = jnp.concatenate([xs[r, pl.ds(PAD + a, w), :] for r in mine[d]], axis=1)
            packed = lax.dot_general(
                block, table[d][:, : len(mine[d]) * LANES], (((1,), (1,)), ((), ())), preferred_element_type=jnp.float32
            )
            for p in range(slots):
                send[d, p, pl.ds(a, w), :] = packed[:, p * LANES : (p + 1) * LANES].astype(jnp.bfloat16)

    def unpack(a, w):
        for d in range(2):
            block = jnp.concatenate([recv[d, p, pl.ds(a, w), :] for p in range(slots)], axis=1)
            found = jnp.dot(block, table[d][:, : len(mine[d]) * LANES], preferred_element_type=jnp.float32)
            for h, r in enumerate(theirs[d]):
                xs[r, pl.ds(a, w), :] = found[:, h * LANES : (h + 1) * LANES].astype(jnp.bfloat16)

    def halo(d, a, w, to):
        if slots:
            return send.at[d, :, pl.ds(a, w), :], recv.at[d, :, pl.ds(to, w), :]
        r0, count = ((rows, TOP), (TOP, BOT))[d]
        s0 = (0, TOP + rows)[d]
        return xs.at[pl.ds(r0, count), pl.ds(PAD + a, w), :], xs.at[pl.ds(s0, count), pl.ds(to, w), :]

    def remote(src, dst, ssem, rsem, to):
        return pltpu.make_async_remote_copy(
            src_ref=src, dst_ref=dst, send_sem=ssem, recv_sem=rsem, device_id=to, device_id_type=MESH
        )

    xto = (xp, xm)
    x_copies = [
        [
            remote(*halo(d, edges[k], edges[k + 1] - edges[k], PAD + edges[k]), x_send.at[d, k], x_recv.at[d, k], (xto[d], gy))
            for d in range(2)
        ]
        for k in range(n)
    ]
    y_copies = [
        remote(
            x_hbm.at[:, pl.ds((cols - PAD, 0)[s], PAD), :],
            xs.at[pl.ds(TOP, rows), pl.ds((0, PAD + cols)[s], PAD), :],
            y_send.at[s], y_recv.at[s], (gx, (yp, ym)[s]),
        )
        for s in range(2)
    ]
    c_copies = [
        [
            remote(*halo(d, (cols - PAD, 0)[s], PAD, (0, PAD + cols)[s]), c_send.at[d, s], c_recv.at[d, s], (xto[d], (yp, ym)[s]))
            for d in range(2)
        ]
        for s in range(2)
    ]

    loads[0].wait()
    loads[1].wait()
    if slots:
        pack(0)
    pl.semaphore_wait(barrier, 8)
    for k in range(n):
        if slots and k:
            pack(k)
        for c in x_copies[k]:
            c.start()
        if k == 0:
            for c in y_copies:
                c.start()
            for c in c_copies[1]:
                c.start()
        if k == n - 1:
            for c in c_copies[0]:
                c.start()
    loads[2].wait()

    def x_tiles(first, last, low, high, t0, t1):
        def step(t, carry):
            x_tile(xs, mid, pl.multiple_of(t * 16, 16), unit, wx, first, last, low, high)
            return carry

        lax.fori_loop(t0, t1, step, 0)

    def y_rows(row_of, count, start, width):
        def step(q, carry):
            y_row(mid, out, row_of(q), start, width, strip.at[q & 1], turn, minus, plus, wy)
            return carry

        lax.fori_loop(0, count, step, 0)

    inner0, inner1 = TOP, rows - BOT
    for c in y_copies:
        c.wait_recv()
    x_tiles(inner0, inner1, TOP, TOP + rows - 1, 0, (cols + 2 * PAD) // 16)
    for k in range(cols // STEP):
        y_rows(lambda q: q + inner0, inner1 - inner0, k * STEP, STEP)

    for k in range(n):
        for c in x_copies[k]:
            c.wait_recv()
        for s in range(2):
            if k == (0, n - 1)[s]:
                for c in c_copies[s]:
                    c.wait_recv()
        a = 0 if k == 0 else PAD + edges[k]
        b = PAD + edges[k + 1] if k < n - 1 else cols + 2 * PAD
        if slots:
            unpack(a, b - a)
        top = TOP + rows + BOT - 1
        x_tiles(0, inner0, 0, top, a // 16, b // 16)
        x_tiles(inner1, rows, 0, top, a // 16, b // 16)
        y_rows(lambda q: q, inner0, k * STEP, STEP)
        y_rows(lambda q: q + inner1, rows - inner1, k * STEP, STEP)

    for group in (*x_copies, y_copies, *c_copies):
        for c in group:
            c.wait_send()


def exchange_and_sweep(slots, collective_id, nx, ny, cells, sx, sy, fx, fy):
    rows, cols, lanes = cells.shape
    n = cols // STEP
    dma = pltpu.SemaphoreType.DMA
    scratch = [
        pltpu.VMEM((rows + TOP + BOT, cols + 2 * PAD, lanes), jnp.bfloat16),
        pltpu.VMEM((rows, cols + 2 * PAD, lanes), jnp.float32),
        pltpu.VMEM((2, STEP + 16, lanes), jnp.float32),
    ]
    if slots:
        scratch += [
            pltpu.VMEM((2, slots * lanes, TOP * lanes), jnp.bfloat16),
            pltpu.VMEM((2, slots, cols, lanes), jnp.bfloat16),
            pltpu.VMEM((2, slots, cols + 2 * PAD, lanes), jnp.bfloat16),
        ]
    scratch += [dma((3,)), dma((2, n)), dma((2, n)), dma((2,)), dma((2,)), dma((2, 2)), dma((2, 2))]
    vmem = pl.BlockSpec(memory_space=pltpu.VMEM)
    return pl.pallas_call(
        functools.partial(kernel, (rows, cols, nx, ny), slots),
        out_shape=jax.ShapeDtypeStruct((rows, cols, lanes), jnp.float32),
        in_specs=[pl.BlockSpec(memory_space=pl.ANY)] + [vmem] * 4,
        out_specs=vmem,
        scratch_shapes=scratch,
        compiler_params=pltpu.CompilerParams(
            vmem_limit_bytes=56 * 1024 * 1024, collective_id=collective_id, has_side_effects=True
        ),
    )(cells, *(a.reshape(1, lanes) for a in (sx, sy, fx, fy)))


def solution(mesh):
    nx, ny = mesh.shape["gx"], mesh.shape["gy"]
    return jax.shard_map(
        functools.partial(exchange_and_sweep, 0, 0, nx, ny),
        mesh=mesh,
        in_specs=(P("gx", "gy", None), P(), P(), P(), P()),
        out_specs=P("gx", "gy", None),
        check_vma=False,
    )
```

```python
import functools
import jax
import jax.numpy as jnp
from jax import lax
from jax.experimental import pallas as pl
from jax.experimental.pallas import tpu as pltpu
from jax.sharding import PartitionSpec as P

REACH = 8
TOP = REACH + 2
BOT = REACH + 1
PAD = 16
LANES = 128
STEP = 128
SLOTS = 4
CHUNKS = 4
MESH = pl.DeviceIdType.MESH


def lagrange(t):
    return (
        -t * (t - 1.0) * (t - 2.0) / 6.0,
        (t + 1.0) * (t - 1.0) * (t - 2.0) / 2.0,
        -(t + 1.0) * t * (t - 2.0) / 2.0,
        (t + 1.0) * t * (t - 1.0) / 6.0,
    )


def rows_needed(shift):
    return jnp.clip(2 - shift, 0, TOP), jnp.clip(shift + 1, 0, BOT)


def build_table(table, count, depth, slots):
    f32 = jnp.float32
    need = count.astype(f32)
    wide = jnp.broadcast_to(need, (16, LANES))
    level = lax.broadcasted_iota(jnp.int32, (16, LANES), 0).astype(f32)
    inside = wide > level
    before = jnp.sum(jnp.minimum(wide, level), axis=1, keepdims=True)
    row = lax.broadcasted_iota(jnp.int32, (LANES, LANES), 0)
    col = lax.broadcasted_iota(jnp.int32, (LANES, LANES), 1)
    upper = jnp.where(row < col, 1.0, 0.0).astype(jnp.bfloat16)
    rank = jnp.dot(
        jnp.where(inside, 1.0, 0.0).astype(jnp.bfloat16), upper, preferred_element_type=f32
    )
    place = jnp.where(inside, before + rank, -1.0)
    lane = row.astype(f32)
    for h in range(depth):
        line = jnp.broadcast_to(place[h : h + 1, :], (LANES, LANES))
        for p in range(slots):
            hit = jnp.where(line == lane + float(p * LANES), 1.0, 0.0)
            table[p * LANES : (p + 1) * LANES, h * LANES : (h + 1) * LANES] = hit.astype(jnp.bfloat16)


def chunk_edges(total):
    tiles = total // 16
    return [16 * (tiles * k // CHUNKS) for k in range(CHUNKS + 1)]


def x_tile(xs, mid, y, to, unit, wx, first, last, low, high):
    m16 = unit >= 16.0
    m8 = unit >= 8.0
    left = jnp.where(m16, unit - 16.0, jnp.where(m8, unit - 8.0, unit))
    m4 = left >= 4.0
    left = jnp.where(m4, left - 4.0, left)
    m2 = left >= 2.0
    left = jnp.where(m2, left - 2.0, left)
    m1 = left >= 1.0

    def source(r):
        return xs[min(max(r, low), high), pl.ds(y, 16), :]

    @functools.cache
    def by8(j):
        return jnp.where(m16, source(j + 16), jnp.where(m8, source(j + 8), source(j)))

    @functools.cache
    def by4(j):
        return jnp.where(m4, by8(j + 4), by8(j))

    @functools.cache
    def by2(j):
        return jnp.where(m2, by4(j + 2), by4(j))

    @functools.cache
    def by1(j):
        return jnp.where(m1, by2(j + 1), by2(j)).astype(jnp.float32)

    for i in range(first, last):
        mid[i, pl.ds(to, 16), :] = (
            wx[0] * by1(i + 3) + wx[1] * by1(i + 2) + wx[2] * by1(i + 1) + wx[3] * by1(i)
        )


def y_row(mid, out, i, start, count, strip, turn, minus, plus, wy):
    tiles = count // 8
    base = start + PAD

    @functools.cache
    def turned(j):
        return jnp.take_along_axis(mid[i, pl.ds(base + 8 * j, 8), :], turn, axis=0)

    for j in range(-1, tiles + 1):
        strip[pl.ds(8 * (j + 1), 8), :] = jnp.where(
            minus, turned(j - 1), jnp.where(plus, turned(j + 1), turned(j))
        )
    for j in range(tiles):
        b = 8 * (j + 1)
        out[i, pl.ds(start + 8 * j, 8), :] = (
            wy[0] * strip[pl.ds(b + 1, 8), :]
            + wy[1] * strip[pl.ds(b, 8), :]
            + wy[2] * strip[pl.ds(b - 1, 8), :]
            + wy[3] * strip[pl.ds(b - 2, 8), :]
        )


def exchange(dims, slots, x_hbm, sx_hbm, sy_hbm, fx_hbm, mid, load, sx_ref, sy_ref, fx_ref, xs, y_out, y_in, *rest):
    rows, cols, nx, ny = dims
    if slots:
        table, send, recv, y_table, y_send_buf, y_recv_buf, load_sem, x_send, x_recv, y_send, y_recv = rest
    else:
        load_sem, x_send, x_recv, y_send, y_recv = rest
    gx, gy = lax.axis_index("gx"), lax.axis_index("gy")
    xm, xp = lax.rem(gx + nx - 1, nx), lax.rem(gx + 1, nx)
    ym, yp = lax.rem(gy + ny - 1, ny), lax.rem(gy + 1, ny)
    total = cols + 2 * PAD

    loads = [
        pltpu.make_async_copy(x_hbm.at[pl.ds(a, c)], xs.at[pl.ds(TOP + a, c), pl.ds(0, cols), :], load_sem.at[k])
        for k, (a, c) in enumerate(((rows - TOP, TOP), (0, TOP), (TOP, rows - 2 * TOP)))
    ]
    y_loads = [
        pltpu.make_async_copy(x_hbm.at[:, pl.ds((0, cols - PAD)[s], PAD), :], y_out.at[s], load_sem.at[3 + s])
        for s in range(2)
    ]
    small = [
        pltpu.make_async_copy(src, dst, load_sem.at[5 + k])
        for k, (src, dst) in enumerate(((sx_hbm, sx_ref), (sy_hbm, sy_ref), (fx_hbm, fx_ref)))
    ]
    for c in (*small, loads[0], loads[1], *y_loads, loads[2]):
        c.start()
    barrier = pltpu.get_barrier_semaphore()
    for to in ((xm, gy), (xp, gy), (gx, ym), (gx, yp)):
        pl.semaphore_signal(barrier, inc=1, device_id=to, device_id_type=MESH)

    for c in small:
        c.wait()
    if slots:
        for d, need in enumerate(rows_needed(sx_ref[...])):
            build_table(table.at[d], need, (TOP, BOT)[d], slots)
    unit = jnp.broadcast_to((sx_ref[...] + REACH).astype(jnp.float32), (16, LANES)).astype(jnp.bfloat16)
    wx = [jnp.broadcast_to(w, (16, LANES)) for w in lagrange(fx_ref[...])]

    edges = chunk_edges(total)
    n = len(edges) - 1
    mine = ([rows - 1 - h + TOP for h in range(TOP)], [TOP + h for h in range(BOT)])
    theirs = ([TOP - 1 - h for h in range(TOP)], [TOP + rows + h for h in range(BOT)])

    def squeeze(lines, lookup, to):
        block = jnp.concatenate(lines, axis=1)
        packed = lax.dot_general(
            block, lookup[:, : len(lines) * LANES], (((1,), (1,)), ((), ())), preferred_element_type=jnp.float32
        )
        for p in range(slots):
            to(p, packed[:, p * LANES : (p + 1) * LANES].astype(jnp.bfloat16))

    def spread(packed, lookup, depth):
        found = jnp.dot(jnp.concatenate(packed, axis=1), lookup[:, : depth * LANES], preferred_element_type=jnp.float32)
        return [found[:, h * LANES : (h + 1) * LANES] for h in range(depth)]

    def pack(k, d):
        a, w = edges[k], edges[k + 1] - edges[k]

        def put(p, value):
            send[d, p, pl.ds(a, w), :] = value

        squeeze([xs[r, pl.ds(a, w), :] for r in mine[d]], table[d], put)

    def pack_y(s):
        def put(p, value):
            y_send_buf[s, p] = value

        by_column = jnp.swapaxes(y_out[s].astype(jnp.float32), 0, 1).astype(jnp.bfloat16)
        order = ([h for h in range(BOT)], [PAD - 1 - h for h in range(TOP)])[s]
        squeeze([by_column[j] for j in order], y_table[s], put)

    def unpack_y(s):
        depth = (BOT, TOP)[s]
        lines = spread([y_recv_buf[s, p] for p in range(slots)], y_table[s], depth)
        zero = jnp.zeros_like(lines[0])
        lines = lines + [zero] * (PAD - depth)
        block = jnp.stack(lines if s == 0 else lines[::-1], axis=0)
        y_in[s] = jnp.swapaxes(block, 0, 1).astype(jnp.bfloat16)

    def unpack(k):
        a, w = edges[k], edges[k + 1] - edges[k]
        for d in range(2):
            lines = spread([recv[d, p, pl.ds(a, w), :] for p in range(slots)], table[d], len(theirs[d]))
            for r, line in zip(theirs[d], lines):
                xs[r, pl.ds(a, w), :] = line.astype(jnp.bfloat16)

    def halo(d, k):
        part = pl.ds(edges[k], edges[k + 1] - edges[k])
        if slots:
            return send.at[d, :, part, :], recv.at[d, :, part, :]
        r0, c = ((rows, TOP), (TOP, BOT))[d]
        return xs.at[pl.ds(r0, c), part, :], xs.at[pl.ds((0, TOP + rows)[d], c), part, :]

    def remote(src, dst, ssem, rsem, to):
        return pltpu.make_async_remote_copy(
            src_ref=src, dst_ref=dst, send_sem=ssem, recv_sem=rsem, device_id=to, device_id_type=MESH
        )

    x_copies = [
        [remote(*halo(d, k), x_send.at[d, k], x_recv.at[d, k], ((xp, xm)[d], gy)) for d in range(2)] for k in range(n)
    ]
    y_from, y_to = (y_send_buf, y_recv_buf) if slots else (y_out, y_in)
    y_copies = [remote(y_from.at[s], y_to.at[s], y_send.at[s], y_recv.at[s], (gx, (ym, yp)[s])) for s in range(2)]

    loads[0].wait()
    if slots:
        pack(0, 0)
    pl.semaphore_wait(barrier, 4)
    x_copies[0][0].start()
    loads[1].wait()
    if slots:
        pack(0, 1)
    x_copies[0][1].start()
    for c in y_loads:
        c.wait()
    if slots:
        for s, need in enumerate(rows_needed(sy_ref[...])[::-1]):
            build_table(y_table.at[s], need, (BOT, TOP)[s], slots)
            pack_y(s)
    for c in y_copies:
        c.start()
    for k in range(1, n):
        if k == n - 1:
            loads[2].wait()
            for s in range(2):
                y_copies[s].wait_recv()
                if slots:
                    unpack_y(s)
                xs[TOP : TOP + rows, cols + PAD * s : cols + PAD * (s + 1), :] = y_in[s]
        for d in range(2):
            if slots:
                pack(k, d)
            x_copies[k][d].start()

    def x_tiles(first, last, low, high, t0, t1):
        def step(t, carry):
            y = pl.multiple_of(t * 16, 16)
            to = pl.multiple_of(lax.rem(t + 1, total // 16) * 16, 16)
            x_tile(xs, mid, y, to, unit, wx, first, last, low, high)
            return carry

        lax.fori_loop(t0, t1, step, 0)

    needs = [jnp.sum(need.astype(jnp.float32)) for ref in (sx_ref, sy_ref) for need in rows_needed(ref[...])]
    load[0] = functools.reduce(jnp.maximum, needs)

    inner0, inner1 = TOP, rows - BOT
    x_tiles(inner0, inner1, TOP, TOP + rows - 1, 0, total // 16)

    top = TOP + rows + BOT - 1
    for k in range(n):
        for c in x_copies[k]:
            c.wait_recv()
        if slots:
            unpack(k)
        x_tiles(0, inner0, 0, top, edges[k] // 16, edges[k + 1] // 16)
        x_tiles(inner1, rows, 0, top, edges[k] // 16, edges[k + 1] // 16)

    for group in (*x_copies, y_copies):
        for c in group:
            c.wait_send()


def finish(dims, mid, sy_ref, fy_ref, out, strip, rows_out, sem):
    rows, cols = dims
    wy = [jnp.broadcast_to(w, (8, LANES)) for w in lagrange(fy_ref[...])]
    tot = lax.broadcasted_iota(jnp.int32, (8, LANES), 0) + jnp.broadcast_to(sy_ref[...], (8, LANES))
    turn, minus, plus = (tot + 16) & 7, tot < 0, tot >= 8
    per = cols // STEP

    def drain(i):
        return pltpu.make_async_copy(rows_out.at[i], out.at[i], sem.at[i])

    def step(i, carry):
        for k in range(per):
            y_row(mid, rows_out, i, k * STEP, STEP, strip.at[k % 2], turn, minus, plus, wy)
        drain(i).start()
        return carry

    lax.fori_loop(0, rows, step, 0)

    def end(i, carry):
        drain(i).wait()
        return carry

    lax.fori_loop(0, rows, end, 0)


def sweep_x(slots, collective_id, nx, ny, cells, sx, sy, fx):
    rows, cols, lanes = cells.shape
    n, total = CHUNKS, cols + 2 * PAD
    dma = pltpu.SemaphoreType.DMA
    bf16 = jnp.bfloat16
    scratch = [
        pltpu.VMEM((1, lanes), jnp.int32),
        pltpu.VMEM((1, lanes), jnp.int32),
        pltpu.VMEM((1, lanes), jnp.float32),
        pltpu.VMEM((rows + TOP + BOT, total, lanes), bf16),
        pltpu.VMEM((2, rows, PAD, lanes), bf16),
        pltpu.VMEM((2, rows, PAD, lanes), bf16),
    ]
    if slots:
        scratch += [
            pltpu.VMEM((2, slots * lanes, TOP * lanes), bf16),
            pltpu.VMEM((2, slots, total, lanes), bf16),
            pltpu.VMEM((2, slots, total, lanes), bf16),
            pltpu.VMEM((2, slots * lanes, TOP * lanes), bf16),
            pltpu.VMEM((2, slots, rows, lanes), bf16),
            pltpu.VMEM((2, slots, rows, lanes), bf16),
        ]
    scratch += [dma((8,)), dma((2, n)), dma((2, n)), dma((2,)), dma((2,))]
    vmem = pl.BlockSpec(memory_space=pltpu.VMEM)
    return pl.pallas_call(
        functools.partial(exchange, (rows, cols, nx, ny), slots),
        out_shape=(
            pltpu.VMEM((rows, total, lanes), jnp.float32),
            jax.ShapeDtypeStruct((1,), jnp.float32),
        ),
        in_specs=[pl.BlockSpec(memory_space=pltpu.HBM)] * 4,
        out_specs=(vmem, pl.BlockSpec(memory_space=pltpu.SMEM)),
        scratch_shapes=scratch,
        compiler_params=pltpu.CompilerParams(
            vmem_limit_bytes=52 * 1024 * 1024, collective_id=collective_id, has_side_effects=True
        ),
    )(cells, sx, sy, fx)


def sweep_y(mid, sy, fy):
    rows, total, lanes = mid.shape
    cols = total - 2 * PAD
    dma = pltpu.SemaphoreType.DMA
    vmem = pl.BlockSpec(memory_space=pltpu.VMEM)
    return pl.pallas_call(
        functools.partial(finish, (rows, cols)),
        out_shape=pltpu.HBM((rows, cols, lanes), jnp.float32),
        in_specs=[vmem] * 3,
        out_specs=pl.BlockSpec(memory_space=pltpu.HBM),
        scratch_shapes=[
            pltpu.VMEM((2, STEP + 16, lanes), jnp.float32),
            pltpu.VMEM((rows, cols, lanes), jnp.float32),
            dma((rows,)),
        ],
        compiler_params=pltpu.CompilerParams(vmem_limit_bytes=24 * 1024 * 1024),
    )(mid, sy, fy)


def body(nx, ny, cells, sx, sy, fx, fy):
    sx, sy, fx, fy = (a.reshape(1, LANES) for a in (sx, sy, fx, fy))
    mid, load = sweep_x(SLOTS, 0, nx, ny, cells, sx, sy, fx)

    out = sweep_y(mid, sy, fy)

    def whole(out):
        return sweep_y(sweep_x(0, 1, nx, ny, cells, sx, sy, fx)[0], sy, fy)

    return lax.cond(load[0] <= SLOTS * LANES, lambda out: out, whole, out)


def solution(mesh):
    return jax.shard_map(
        functools.partial(body, mesh.shape["gx"], mesh.shape["gy"]),
        mesh=mesh,
        in_specs=(P("gx", "gy", None), P(), P(), P(), P()),
        out_specs=P("gx", "gy", None),
        check_vma=False,
    )
```

```python
import functools
import jax
import jax.numpy as jnp
from jax import lax
from jax.experimental import pallas as pl
from jax.experimental.pallas import tpu as pltpu
from jax.sharding import PartitionSpec as P

REACH = 8
TOP = REACH + 2
BOT = REACH + 1
PAD = 16
LANES = 128
STEP = 128
SLOTS = 4
CHUNKS = 4
MESH = pl.DeviceIdType.MESH


def lagrange(t):
    return (
        -t * (t - 1.0) * (t - 2.0) / 6.0,
        (t + 1.0) * (t - 1.0) * (t - 2.0) / 2.0,
        -(t + 1.0) * t * (t - 2.0) / 2.0,
        (t + 1.0) * t * (t - 1.0) / 6.0,
    )


def rows_needed(shift):
    return jnp.clip(2 - shift, 0, TOP), jnp.clip(shift + 1, 0, BOT)


def build_table(table, count, depth, slots):
    f32 = jnp.float32
    need = count.astype(f32)
    wide = jnp.broadcast_to(need, (16, LANES))
    level = lax.broadcasted_iota(jnp.int32, (16, LANES), 0).astype(f32)
    inside = wide > level
    before = jnp.sum(jnp.minimum(wide, level), axis=1, keepdims=True)
    row = lax.broadcasted_iota(jnp.int32, (LANES, LANES), 0)
    col = lax.broadcasted_iota(jnp.int32, (LANES, LANES), 1)
    upper = jnp.where(row < col, 1.0, 0.0).astype(jnp.bfloat16)
    rank = jnp.dot(
        jnp.where(inside, 1.0, 0.0).astype(jnp.bfloat16), upper, preferred_element_type=f32
    )
    place = jnp.where(inside, before + rank, -1.0)
    bf16 = jnp.bfloat16
    lane = lax.broadcasted_iota(jnp.int32, (16, LANES), 0).astype(f32)
    lanes = [(lane + float(a)).astype(bf16) for a in range(0, LANES, 16)]
    one, zero = jnp.ones((16, LANES), bf16), jnp.zeros((16, LANES), bf16)
    for p in range(slots):
        local = place - float(p * LANES)
        local = jnp.where((local >= 0.0) & (local < float(LANES)), local, -1.0)
        for h in range(depth):
            line = jnp.broadcast_to(local[h : h + 1, :], (16, LANES)).astype(bf16)
            for m, value in enumerate(lanes):
                table[pl.ds(p * LANES + 16 * m, 16), h * LANES : (h + 1) * LANES] = jnp.where(line == value, one, zero)


def chunk_edges(total):
    tiles = total // 16
    return [16 * (tiles * k // CHUNKS) for k in range(CHUNKS + 1)]


def x_tile(xs, mid, y, to, unit, wx, first, last, low, high):
    m16 = unit >= 16.0
    m8 = unit >= 8.0
    left = jnp.where(m16, unit - 16.0, jnp.where(m8, unit - 8.0, unit))
    m4 = left >= 4.0
    left = jnp.where(m4, left - 4.0, left)
    m2 = left >= 2.0
    left = jnp.where(m2, left - 2.0, left)
    m1 = left >= 1.0

    def source(r):
        return xs[min(max(r, low), high), pl.ds(y, 16), :]

    @functools.cache
    def by8(j):
        return jnp.where(m16, source(j + 16), jnp.where(m8, source(j + 8), source(j)))

    @functools.cache
    def by4(j):
        return jnp.where(m4, by8(j + 4), by8(j))

    @functools.cache
    def by2(j):
        return jnp.where(m2, by4(j + 2), by4(j))

    @functools.cache
    def by1(j):
        return jnp.where(m1, by2(j + 1), by2(j)).astype(jnp.float32)

    for i in range(first, last):
        mid[i, pl.ds(to, 16), :] = (
            wx[0] * by1(i + 3) + wx[1] * by1(i + 2) + wx[2] * by1(i + 1) + wx[3] * by1(i)
        )


def y_row(mid, out, i, start, count, strip, turn, minus, plus, wy):
    tiles = count // 8
    base = start + PAD

    @functools.cache
    def turned(j):
        return jnp.take_along_axis(mid[i, pl.ds(base + 8 * j, 8), :], turn, axis=0)

    aligned = {}
    for j in range(-1, tiles + 1):
        aligned[j] = jnp.where(minus, turned(j - 1), jnp.where(plus, turned(j + 1), turned(j)))
        strip[pl.ds(8 * (j + 1), 8), :] = aligned[j]
        if j < 1:
            continue
        b = 8 * j
        out[i, pl.ds(start + 8 * (j - 1), 8), :] = (
            wy[0] * strip[pl.ds(b + 1, 8), :]
            + wy[1] * aligned[j - 1]
            + wy[2] * strip[pl.ds(b - 1, 8), :]
            + wy[3] * strip[pl.ds(b - 2, 8), :]
        )


def exchange(dims, slots, x_hbm, sx_hbm, sy_hbm, fx_hbm, fy_hbm, mid, load, sy_ref, fy_ref, sx_ref, fx_ref, xs, y_out, y_in, *rest):
    rows, cols, nx, ny = dims
    if slots:
        table, send, recv, y_table, y_send_buf, y_recv_buf, load_sem, x_send, x_recv, y_send, y_recv = rest
    else:
        load_sem, x_send, x_recv, y_send, y_recv = rest
    gx, gy = lax.axis_index("gx"), lax.axis_index("gy")
    xm, xp = lax.rem(gx + nx - 1, nx), lax.rem(gx + 1, nx)
    ym, yp = lax.rem(gy + ny - 1, ny), lax.rem(gy + 1, ny)
    total = cols + 2 * PAD

    loads = [
        pltpu.make_async_copy(x_hbm.at[pl.ds(a, c)], xs.at[pl.ds(TOP + a, c), pl.ds(0, cols), :], load_sem.at[k])
        for k, (a, c) in enumerate(((rows - TOP, TOP), (0, TOP), (TOP, rows - 2 * TOP)))
    ]
    y_loads = [
        pltpu.make_async_copy(x_hbm.at[:, pl.ds((0, cols - PAD)[s], PAD), :], y_out.at[s], load_sem.at[3 + s])
        for s in range(2)
    ]
    small = [
        pltpu.make_async_copy(src, dst, load_sem.at[5 + k])
        for k, (src, dst) in enumerate(((sx_hbm, sx_ref), (fx_hbm, fx_ref), (sy_hbm, sy_ref), (fy_hbm, fy_ref)))
    ]
    for c in (*small, loads[0], loads[1], *y_loads, loads[2]):
        c.start()
    barrier = pltpu.get_barrier_semaphore()
    for to in ((xm, gy), (xp, gy), (gx, ym), (gx, yp)):
        pl.semaphore_signal(barrier, inc=1, device_id=to, device_id_type=MESH)

    for c in small:
        c.wait()
    if slots:
        for d, need in enumerate(rows_needed(sx_ref[...])):
            build_table(table.at[d], need, (TOP, BOT)[d], slots)
    unit = jnp.broadcast_to((sx_ref[...] + REACH).astype(jnp.float32), (16, LANES)).astype(jnp.bfloat16)
    wx = [jnp.broadcast_to(w, (16, LANES)) for w in lagrange(fx_ref[...])]

    edges = chunk_edges(total)
    n = len(edges) - 1
    mine = ([rows - 1 - h + TOP for h in range(TOP)], [TOP + h for h in range(BOT)])
    theirs = ([TOP - 1 - h for h in range(TOP)], [TOP + rows + h for h in range(BOT)])

    def squeeze(lines, lookup, to):
        block = jnp.concatenate(lines, axis=1)
        packed = lax.dot_general(
            block, lookup[:, : len(lines) * LANES], (((1,), (1,)), ((), ())), preferred_element_type=jnp.float32
        )
        for p in range(slots):
            to(p, packed[:, p * LANES : (p + 1) * LANES].astype(jnp.bfloat16))

    def spread(packed, lookup, depth):
        found = jnp.dot(jnp.concatenate(packed, axis=1), lookup[:, : depth * LANES], preferred_element_type=jnp.float32)
        return [found[:, h * LANES : (h + 1) * LANES] for h in range(depth)]

    def pack(k, d):
        a, w = edges[k], edges[k + 1] - edges[k]

        def put(p, value):
            send[d, p, pl.ds(a, w), :] = value

        squeeze([xs[r, pl.ds(a, w), :] for r in mine[d]], table[d], put)

    def pack_y(s):
        def put(p, value):
            y_send_buf[s, p] = value

        by_column = jnp.swapaxes(y_out[s].astype(jnp.float32), 0, 1).astype(jnp.bfloat16)
        order = ([h for h in range(BOT)], [PAD - 1 - h for h in range(TOP)])[s]
        squeeze([by_column[j] for j in order], y_table[s], put)

    def unpack_y(s):
        depth = (BOT, TOP)[s]
        lines = spread([y_recv_buf[s, p] for p in range(slots)], y_table[s], depth)
        zero = jnp.zeros_like(lines[0])
        lines = lines + [zero] * (PAD - depth)
        block = jnp.stack(lines if s == 0 else lines[::-1], axis=0)
        y_in[s] = jnp.swapaxes(block, 0, 1).astype(jnp.bfloat16)

    def unpack(k):
        a, w = edges[k], edges[k + 1] - edges[k]
        for d in range(2):
            lines = spread([recv[d, p, pl.ds(a, w), :] for p in range(slots)], table[d], len(theirs[d]))
            for r, line in zip(theirs[d], lines):
                xs[r, pl.ds(a, w), :] = line.astype(jnp.bfloat16)

    def halo(d, k):
        part = pl.ds(edges[k], edges[k + 1] - edges[k])
        if slots:
            return send.at[d, :, part, :], recv.at[d, :, part, :]
        r0, c = ((rows, TOP), (TOP, BOT))[d]
        return xs.at[pl.ds(r0, c), part, :], xs.at[pl.ds((0, TOP + rows)[d], c), part, :]

    def remote(src, dst, ssem, rsem, to):
        return pltpu.make_async_remote_copy(
            src_ref=src, dst_ref=dst, send_sem=ssem, recv_sem=rsem, device_id=to, device_id_type=MESH
        )

    x_copies = [
        [remote(*halo(d, k), x_send.at[d, k], x_recv.at[d, k], ((xp, xm)[d], gy)) for d in range(2)] for k in range(n)
    ]
    y_from, y_to = (y_send_buf, y_recv_buf) if slots else (y_out, y_in)
    y_copies = [remote(y_from.at[s], y_to.at[s], y_send.at[s], y_recv.at[s], (gx, (ym, yp)[s])) for s in range(2)]

    def x_tiles(first, last, low, high, t0, t1):
        def step(t, carry):
            y = pl.multiple_of(t * 16, 16)
            to = pl.multiple_of(lax.rem(t + 1, total // 16) * 16, 16)
            x_tile(xs, mid, y, to, unit, wx, first, last, low, high)
            return carry

        lax.fori_loop(t0, t1, step, 0)

    inner0, inner1 = TOP, rows - BOT
    loads[0].wait()
    if slots:
        pack(0, 0)
    pl.semaphore_wait(barrier, 4)
    x_copies[0][0].start()
    loads[1].wait()
    if slots:
        pack(0, 1)
    x_copies[0][1].start()
    for c in y_loads:
        c.wait()
    if slots:
        for s, need in enumerate(rows_needed(sy_ref[...])[::-1]):
            build_table(y_table.at[s], need, (BOT, TOP)[s], slots)
            pack_y(s)
    for c in y_copies:
        c.start()
    for k in range(1, n):
        if k == n - 1:
            loads[2].wait()
            x_tiles(inner0, inner1, TOP, TOP + rows - 1, 0, cols // 16)
            for s in range(2):
                y_copies[s].wait_recv()
                if slots:
                    unpack_y(s)
                xs[TOP : TOP + rows, cols + PAD * s : cols + PAD * (s + 1), :] = y_in[s]
        for d in range(2):
            if slots:
                pack(k, d)
            x_copies[k][d].start()

    needs = [jnp.sum(need.astype(jnp.float32)) for ref in (sx_ref, sy_ref) for need in rows_needed(ref[...])]
    load[0] = functools.reduce(jnp.maximum, needs)

    x_tiles(inner0, inner1, TOP, TOP + rows - 1, cols // 16, total // 16)

    top = TOP + rows + BOT - 1
    for k in range(n):
        for c in x_copies[k]:
            c.wait_recv()
        if slots:
            unpack(k)
        x_tiles(0, inner0, 0, top, edges[k] // 16, edges[k + 1] // 16)
        x_tiles(inner1, rows, 0, top, edges[k] // 16, edges[k + 1] // 16)

    for group in (*x_copies, y_copies):
        for c in group:
            c.wait_send()


def finish(dims, mid, sy_ref, fy_ref, out, strip, rows_out, sem):
    rows, cols = dims
    wy = [jnp.broadcast_to(w, (8, LANES)) for w in lagrange(fy_ref[...])]
    tot = lax.broadcasted_iota(jnp.int32, (8, LANES), 0) + jnp.broadcast_to(sy_ref[...], (8, LANES))
    turn, minus, plus = (tot + 16) & 7, tot < 0, tot >= 8
    per = cols // STEP

    def drain(i):
        return pltpu.make_async_copy(rows_out.at[i], out.at[i], sem.at[i])

    def step(i, carry):
        for k in range(per):
            y_row(mid, rows_out, i, k * STEP, STEP, strip.at[k % 2], turn, minus, plus, wy)
        drain(i).start()
        return carry

    lax.fori_loop(0, rows, step, 0)

    def end(i, carry):
        drain(i).wait()
        return carry

    lax.fori_loop(0, rows, end, 0)


def sweep_x(slots, collective_id, nx, ny, cells, sx, sy, fx, fy):
    rows, cols, lanes = cells.shape
    n, total = CHUNKS, cols + 2 * PAD
    dma = pltpu.SemaphoreType.DMA
    bf16 = jnp.bfloat16
    scratch = [
        pltpu.VMEM((1, lanes), jnp.int32),
        pltpu.VMEM((1, lanes), jnp.float32),
        pltpu.VMEM((rows + TOP + BOT, total, lanes), bf16),
        pltpu.VMEM((2, rows, PAD, lanes), bf16),
        pltpu.VMEM((2, rows, PAD, lanes), bf16),
    ]
    if slots:
        scratch += [
            pltpu.VMEM((2, slots * lanes, TOP * lanes), bf16),
            pltpu.VMEM((2, slots, total, lanes), bf16),
            pltpu.VMEM((2, slots, total, lanes), bf16),
            pltpu.VMEM((2, slots * lanes, TOP * lanes), bf16),
            pltpu.VMEM((2, slots, rows, lanes), bf16),
            pltpu.VMEM((2, slots, rows, lanes), bf16),
        ]
    scratch += [dma((9,)), dma((2, n)), dma((2, n)), dma((2,)), dma((2,))]
    vmem = pl.BlockSpec(memory_space=pltpu.VMEM)
    return pl.pallas_call(
        functools.partial(exchange, (rows, cols, nx, ny), slots),
        out_shape=(
            pltpu.VMEM((rows, total, lanes), jnp.float32),
            jax.ShapeDtypeStruct((1,), jnp.float32),
            pltpu.VMEM((1, lanes), jnp.int32),
            pltpu.VMEM((1, lanes), jnp.float32),
        ),
        in_specs=[pl.BlockSpec(memory_space=pltpu.HBM)] * 5,
        out_specs=(vmem, pl.BlockSpec(memory_space=pltpu.SMEM), vmem, vmem),
        scratch_shapes=scratch,
        compiler_params=pltpu.CompilerParams(
            vmem_limit_bytes=52 * 1024 * 1024, collective_id=collective_id, has_side_effects=True
        ),
    )(cells, sx, sy, fx, fy)


def sweep_y(mid, sy, fy):
    rows, total, lanes = mid.shape
    cols = total - 2 * PAD
    dma = pltpu.SemaphoreType.DMA
    vmem = pl.BlockSpec(memory_space=pltpu.VMEM)
    return pl.pallas_call(
        functools.partial(finish, (rows, cols)),
        out_shape=pltpu.HBM((rows, cols, lanes), jnp.float32),
        in_specs=[vmem] * 3,
        out_specs=pl.BlockSpec(memory_space=pltpu.HBM),
        scratch_shapes=[
            pltpu.VMEM((2, STEP + 16, lanes), jnp.float32),
            pltpu.VMEM((rows, cols, lanes), jnp.float32),
            dma((rows,)),
        ],
        compiler_params=pltpu.CompilerParams(vmem_limit_bytes=24 * 1024 * 1024),
    )(mid, sy, fy)


def body(nx, ny, cells, sx, sy, fx, fy):
    sx, sy, fx, fy = (a.reshape(1, LANES) for a in (sx, sy, fx, fy))
    args = (nx, ny, cells, sx, sy, fx, fy)
    mid, load, *along_y = sweep_x(SLOTS, 0, *args)

    out = sweep_y(mid, *along_y)

    def whole(out):
        mid, _, *along_y = sweep_x(0, 1, *args)
        return sweep_y(mid, *along_y)

    return lax.cond(load[0] <= SLOTS * LANES, lambda out: out, whole, out)


def solution(mesh):
    return jax.shard_map(
        functools.partial(body, mesh.shape["gx"], mesh.shape["gy"]),
        mesh=mesh,
        in_specs=(P("gx", "gy", None), P(), P(), P(), P()),
        out_specs=P("gx", "gy", None),
        check_vma=False,
    )
```
